32 devices in a mesh: runs: 8 (over z, y), tp: 4 (over x, core).
Axes of the slice: x: 2, y: 2, z: 4, core: 2. Of those that a mesh axis runs over, the one named last changes fastest.
Arguments:
- hidden: bfloat16 [4096, 8192], P('runs', 'tp'), may hold values from -6 to 6
- cotangent: bfloat16 [4096, 8192], P('runs', 'tp'), may hold values from -0.059814453 to 0.059814453
- rotation: float32 [8192, 512], P(None, 'tp'), may hold values from -0.0625 to 0.0625
- matching: int32 [32], P('runs'), may hold values from 0 to 31
- mask: int32 [32, 128], P('runs'), may hold values 0 or 1
Outputs:
- intervened: bfloat16 [4096, 8192], P('runs', 'tp')
- grad_rotation: float32 [8192, 512], P('runs', 'tp')
The draws below stay inside these ranges and needn't reach their ends.
All inputs are finite; a program needn't handle non-finite values. No bound on the sum of `mask` on one device may be relied on, other than what follows from the above.
Results may differ from the reference program's by a relative error of at most 0.0045.
Values may be sent and summed in bfloat16 or wider, within the bound.
A program may use at most 128 MiB of HBM per device.

```python
import math
import jax
import jax.numpy as jnp
import numpy as np
from jax import lax

D = 8192
K = 512
L = 128
RUNS = 32
TOKENS = 4096


def plant(array, key, least, top_value):
    longest = array.shape.index(max(array.shape))
    spots = []
    for shift in (0, 1):
        where = [jax.random.randint(jax.random.fold_in(key, axis), (), 0, length) for axis, length in enumerate(array.shape)]
        where[longest] = (where[longest] + shift) % array.shape[longest]
        spots.append(tuple(where))
    return array.at[spots[0]].set(least).at[spots[1]].set(top_value)


def levels(stream_key, shape, shards, least, high):
    factor_of = 1.0
    for axis_at, shards_of in shards:
        steps = jax.random.uniform(jax.random.fold_in(jax.random.fold_in(stream_key, 6), axis_at), (shards_of,), jnp.float32, least / len(shards), high / len(shards))
        factor_of = factor_of * jnp.repeat(jnp.exp(steps), shape[axis_at] // shards_of).reshape((-1,) + (1,) * (len(shape) - 1 - axis_at))
    return factor_of


def cumulative_ranks(number_of, skew):
    weights = [(1 << 20) // math.isqrt(grade ** skew) + 1 for grade in range(1, number_of + 1)]
    spread = 1 + sum(weights) // (1 << 30)
    return np.cumsum(np.array([max(1, weight // spread) for weight in weights]))


def skewed_ids(stream_key, shape, number_of, lean):
    table = cumulative_ranks(number_of, lean)
    lot = jax.random.randint(jax.random.fold_in(stream_key, 1), shape, 0, int(table[number_of - 1]))
    standing = jnp.searchsorted(jnp.asarray(table, jnp.int32), lot, side="right")
    return jax.random.permutation(jax.random.fold_in(stream_key, 2), number_of)[standing].astype(jnp.int32)


def scatter_about(key, extent, scale, bound, pieces=(), dtype=jnp.bfloat16):
    values = scale * jax.random.normal(key, extent, jnp.float32)
    if pieces:
        values = values * levels(key, extent, pieces, -0.22, 0.18)
    return jnp.clip(values, -bound, bound).astype(dtype)


def setup_inputs(seed: int = 0) -> dict:
    arg_keys = jax.random.split(jax.random.key(seed), 6)
    return {
        "hidden": scatter_about(arg_keys[0], (TOKENS, D), 1.0, 6.0, ((0, 8), (1, 4))),
        "cotangent": scatter_about(arg_keys[1], (TOKENS, D), 0.01, 0.059814453, ((0, 8), (1, 4))),
        "rotation": scatter_about(arg_keys[2], (D, K), D ** -0.5, 0.0625, ((1, 4),), jnp.float32),
        "matching": plant(skewed_ids(arg_keys[3], (RUNS,), RUNS, 2), jax.random.fold_in(arg_keys[3], 3), 0, RUNS - 1).astype(jnp.int32),
        "mask": plant((jax.random.randint(arg_keys[4], (RUNS, L), 0, 2) < 1).astype(jnp.int32), jax.random.fold_in(arg_keys[4], 1), 0, 1),
    }


def reference(hidden, cotangent, rotation, matching, mask):
    high = lax.Precision.HIGHEST
    wide_hidden = hidden.astype(jnp.float32)
    wide_cotangent = cotangent.astype(jnp.float32)
    coords = jnp.dot(wide_hidden, rotation, precision=high).reshape(RUNS, L, K)
    chosen = mask.astype(jnp.float32)[:, :, None]
    update = (chosen * (coords[matching] - coords)).reshape(TOKENS, K)
    intervened = (wide_hidden + jnp.dot(update, rotation.T, precision=high)).astype(jnp.bfloat16)
    pulled = chosen * jnp.dot(wide_cotangent, rotation, precision=high).reshape(RUNS, L, K)
    returned = jax.ops.segment_sum(pulled, matching, num_segments=RUNS)
    net = (returned - pulled).reshape(TOKENS, K)
    grad_rotation = jnp.dot(wide_cotangent.T, update, precision=high) + jnp.dot(wide_hidden.T, net, precision=high)
    return intervened, grad_rotation
```

```python
import functools

import jax
import jax.numpy as jnp
from jax import lax
from jax.experimental import pallas as pl
from jax.experimental.pallas import tpu as pltpu
from jax.sharding import PartitionSpec as P

F32 = jnp.float32
BF16 = jnp.bfloat16


def kernel(
    R, T, lr, L, rows, hid, cot, rot, mask, matv, match, out, grad,
    x, w, part, prec, own, gath, matg, upd, gkeep, gsend, yrec, zsend, zrec, fin, frec,
    lsem, rsend, rrecv, msend, mrecv, psend, precv, asend, arecv, usend, urecv,
    ysend, yrecv, zsem, zrsem, fsem,
):
    q = R // T
    n, F = hid.shape
    C = rot.shape[1]
    S = F // q
    r = lax.axis_index("runs")
    j = lax.axis_index("tp")
    a = r // q
    b = lax.rem(r, q)
    blk = 2 * lr

    def remote(src, dst, ss, rs, dr, dj):
        return pltpu.make_async_remote_copy(
            src_ref=src, dst_ref=dst, send_sem=ss, recv_sem=rs,
            device_id=(dr, dj), device_id_type=pl.DeviceIdType.MESH,
        )

    def other(i, k, size):
        return lax.rem(i + k, size)

    loads = [
        pltpu.make_async_copy(hid, x.at[0], lsem.at[0]),
        pltpu.make_async_copy(cot, x.at[1], lsem.at[1]),
        pltpu.make_async_copy(
            rot.at[pl.ds(pl.multiple_of(j * F, F), F), :],
            w.at[:, pl.ds(pl.multiple_of(j * C, C), C)], lsem.at[2]),
        pltpu.make_async_copy(matv, matg.at[r], lsem.at[3]),
    ]
    for c in loads:
        c.start()

    barrier = pltpu.get_barrier_semaphore()
    for k in range(1, R):
        pl.semaphore_signal(barrier, inc=1, device_id=(other(r, k, R), j),
                            device_id_type=pl.DeviceIdType.MESH)
    for k in range(1, T):
        pl.semaphore_signal(barrier, inc=1, device_id=(r, other(j, k, T)),
                            device_id_type=pl.DeviceIdType.MESH)

    @pl.when(a != j)
    def _():
        pl.semaphore_signal(barrier, inc=1, device_id=(j * q + b, a),
                            device_id_type=pl.DeviceIdType.MESH)
    pl.semaphore_wait(barrier, R - 1 + T - 1 + jnp.where(a != j, 1, 0).astype(jnp.int32))

    rcopies = []
    for k in range(1, T):
        p = other(j, k, T)
        rcopies.append(remote(
            rot.at[pl.ds(pl.multiple_of(p * F, F), F), :],
            w.at[:, pl.ds(pl.multiple_of(j * C, C), C)],
            rsend.at[p], rrecv.at[j], r, p))
    for c in rcopies:
        c.start()
    mcopies = []
    for k in range(1, R):
        p = other(r, k, R)
        mcopies.append(remote(matv, matg.at[r], msend.at[p], mrecv.at[r], p, j))
    for c in mcopies:
        c.start()
    for c in loads:
        c.wait()
    for k in range(1, T):
        p = other(j, k, T)
        dst = w.at[:, pl.ds(pl.multiple_of(p * C, C), C)]
        remote(rot.at[pl.ds(0, F), :], dst, rsend.at[p], rrecv.at[p], r, p).wait_recv()

    step = L
    for s in range(2):
        def body(i, _, s=s):
            rs = pl.ds(pl.multiple_of(i * step, step), step)
            v = jnp.dot(x[s, rs, :], w[...], preferred_element_type=F32)
            ws = pl.ds(pl.multiple_of(s * n + i * step, step), step)
            for p in range(T):
                part[p, ws, :] = v[:, p * C:(p + 1) * C].astype(BF16)
                @pl.when(j == p)
                def _():
                    own[ws, :] = v[:, p * C:(p + 1) * C]
            return 0
        lax.fori_loop(0, n // step, body, 0)
    pcopies = []
    for k in range(1, T):
        p = other(j, k, T)
        pcopies.append(remote(part.at[p], prec.at[j], psend.at[p], precv.at[j], r, p))
    for c in pcopies:
        c.start()
    for k in range(1, T):
        p = other(j, k, T)
        remote(part.at[p], prec.at[p], psend.at[p], precv.at[p], r, p).wait_recv()
    for i in range(blk):
        rs = pl.ds(i * L, L)
        v = own[rs, :]
        for k in range(1, T):
            v = v + prec[other(j, k, T), rs, :].astype(F32)
        if i >= lr:
            v = v * mask[pl.ds((i - lr) * L, L), :]
        own[rs, :] = v
        gath[r * blk + i] = v.astype(BF16)

    def block(g):
        return gath.at[pl.ds(g * blk, blk)]

    sends = []
    for k in range(1, T):
        p = other(a, k, T)
        sends.append(remote(block(r), block(r), asend.at[p, b], arecv.at[r], p * q + b, j))
    for k in range(1, q):
        p = other(b, k, q)
        sends.append(remote(block(r), block(r), asend.at[a, p], arecv.at[r], a * q + p, j))
    for c in sends:
        c.start()
    for k in range(1, T):
        p = other(a, k, T)
        g = p * q + b
        remote(block(g), block(g), asend.at[p, b], arecv.at[g], g, j).wait_recv()
        for m in range(1, q):
            e = other(b, m, q)
            c = remote(block(g), block(g), asend.at[p, e], arecv.at[g], a * q + e, j)
            c.start()
            sends.append(c)
    for k in range(T):
        p = other(a, k, T)
        for m in range(1, q):
            g = p * q + other(b, m, q)
            remote(block(g), block(g), asend.at[p, b], arecv.at[g], g, j).wait_recv()
    for k in range(1, R):
        p = other(r, k, R)
        remote(matv, matg.at[p], msend.at[p], mrecv.at[p], p, j).wait_recv()

    for i in range(lr):
        rs = pl.ds(i * L, L)
        m = match[i]
        src = gath[m + (m // lr) * lr].astype(F32)
        mine = matg[r, pl.ds(i, 1), :] == (r * lr + i).astype(F32)
        upd[j, rs, :] = jnp.where(mine, 0.0, mask[rs, :] * (src - own[rs, :])).astype(BF16)

        def back(g, acc, i=i):
            for u in range(lr):
                hit = matg[g, pl.ds(u, 1), :] == (r * lr + i).astype(F32)
                acc = acc + jnp.where(hit, gath[g * blk + lr + u].astype(F32), 0.0)
            return acc
        acc = lax.fori_loop(0, R, back, -own[pl.ds((lr + i) * L, L), :])
        for u in range(lr):
            hit = matg[r, pl.ds(u, 1), :] == (r * lr + i).astype(F32)
            full = own[pl.ds((lr + u) * L, L), :]
            acc = acc + jnp.where(hit, full - gath[r * blk + lr + u].astype(F32), 0.0)
        upd[j, pl.ds(n + i * L, L), :] = acc.astype(BF16)
    ucopies = []
    for k in range(1, T):
        p = other(j, k, T)
        ucopies.append(remote(upd.at[j], upd.at[j], usend.at[p], urecv.at[j], r, p))
    for c in ucopies:
        c.start()

    def grads(p):
        def half(e):
            fs = pl.ds(pl.multiple_of(e * S, S), S)
            dims = (((0,), (0,)), ((), ()))
            return (
                lax.dot_general(upd[p, pl.ds(0, n), :], x[1, :, fs], dims, preferred_element_type=F32)
                + lax.dot_general(upd[p, pl.ds(n, n), :], x[0, :, fs], dims, preferred_element_type=F32))
        gkeep[p] = half(b)
        for m in range(1, q):
            e = other(b, m, q)
            gsend[p, e] = half(e).astype(BF16)
            c = remote(gsend.at[p, e], yrec.at[b, p], ysend.at[p, e], yrecv.at[b, p], a * q + e, j)
            c.start()

    order = [other(j, k, T) for k in range(T)]
    for k, p in enumerate(order):
        if k:
            remote(upd.at[p], upd.at[p], usend.at[p], urecv.at[p], r, p).wait_recv()
        grads(p)

    def inter(i, _):
        rs = pl.ds(pl.multiple_of(i * L, L), L)
        u = jnp.concatenate([upd[p, rs, :] for p in range(T)], axis=1)
        v = lax.dot_general(u, w[...], (((1,), (1,)), ((), ())), preferred_element_type=F32)
        out[rs, :] = (x[0, rs, :].astype(F32) + v).astype(BF16)
        return 0

    def ysum(p):
        v = gkeep[p]
        for m in range(1, q):
            e = other(b, m, q)
            remote(gsend.at[p, e], yrec.at[e, p], ysend.at[p, e], yrecv.at[e, p], a * q + e, j).wait_recv()
            v = v + yrec[e, p].astype(F32)
        return v

    for p in order:
        v = ysum(p)

        @pl.when(p == a)
        def _():
            fin[...] = v

        @pl.when(p != a)
        def _():
            zsend[p] = v.astype(BF16)
            remote(zsend.at[p], zrec.at[a], zsem.at[p], zrsem.at[a], p * q + b, j).start()
    lax.fori_loop(0, n // L, inter, 0)
    for k in range(1, T):
        p = other(a, k, T)
        remote(zsend.at[p], zrec.at[p], zsem.at[p], zrsem.at[p], p * q + b, j).wait_recv()
    v = fin[...]
    for k in range(1, T):
        v = v + zrec[other(a, k, T)].astype(F32)
    fin[...] = v

    @pl.when(a != j)
    def _():
        c = remote(fin, frec, fsem.at[0], fsem.at[1], j * q + b, a)
        c.start()
        c.wait()
        grad[...] = frec[...].T

    @pl.when(a == j)
    def _():
        grad[...] = fin[...].T

    for c in rcopies + mcopies + pcopies + sends + ucopies:
        c.wait_send()
    for k in range(T):
        p = other(j, k, T)
        for m in range(1, q):
            e = other(b, m, q)
            remote(gsend.at[p, e], yrec.at[b, p], ysend.at[p, e], yrecv.at[b, p], a * q + e, j).wait_send()
    for k in range(1, T):
        p = other(a, k, T)
        remote(zsend.at[p], zrec.at[a], zsem.at[p], zrsem.at[a], p * q + b, j).wait_send()


def per_device(R, T, hidden, cotangent, rotation, matching, mask):
    n, F = hidden.shape
    D, C = rotation.shape
    lr, L = mask.shape
    q = R // T
    S = F // q
    rows = -(-lr // 8) * 8
    rot = rotation.astype(BF16)
    maskf = jnp.broadcast_to(mask.astype(F32).reshape(n, 1), (n, C))
    matv = jnp.broadcast_to(jnp.pad(matching, (0, rows - lr)).astype(F32)[:, None], (rows, C))
    dma = lambda *s: pltpu.SemaphoreType.DMA(s)
    any_, vm, sm = (pl.BlockSpec(memory_space=m) for m in (pl.ANY, pltpu.VMEM, pltpu.SMEM))
    return pl.pallas_call(
        functools.partial(kernel, R, T, lr, L, rows),
        out_shape=(
            jax.ShapeDtypeStruct((n, F), BF16),
            jax.ShapeDtypeStruct((S, C), F32),
        ),
        in_specs=[any_, any_, any_, vm, vm, sm],
        out_specs=(vm, vm),
        scratch_shapes=[
            pltpu.VMEM((2, n, F), BF16),
            pltpu.VMEM((F, T * C), BF16),
            pltpu.VMEM((T, 2 * n, C), BF16),
            pltpu.VMEM((T, 2 * n, C), BF16),
            pltpu.VMEM((2 * n, C), F32),
            pltpu.VMEM((R * 2 * lr, L, C), BF16),
            pltpu.VMEM((R, rows, C), F32),
            pltpu.VMEM((T, 2 * n, C), BF16),
            pltpu.VMEM((T, C, S), F32),
            pltpu.VMEM((T, q, C, S), BF16),
            pltpu.VMEM((q, T, C, S), BF16),
            pltpu.VMEM((T, C, S), BF16),
            pltpu.VMEM((T, C, S), BF16),
            pltpu.VMEM((C, S), F32),
            pltpu.VMEM((C, S), F32),
            dma(4), dma(T), dma(T), dma(R), dma(R), dma(T), dma(T),
            dma(T, q), dma(R), dma(T), dma(T),
            dma(T, q), dma(q, T), dma(T), dma(T), dma(2),
        ],
        compiler_params=pltpu.CompilerParams(
            collective_id=0, has_side_effects=True, vmem_limit_bytes=60 * 1024 * 1024
        ),
    )(hidden, cotangent, rot, maskf, matv, matching)


def solution(mesh):
    in_specs = (P("runs", "tp"), P("runs", "tp"), P(None, "tp"), P("runs"), P("runs", None))
    out_specs = (P("runs", "tp"), P("runs", "tp"))
    return jax.shard_map(
        functools.partial(per_device, mesh.shape["runs"], mesh.shape["tp"]),
        mesh=mesh, in_specs=in_specs, out_specs=out_specs, check_vma=False,
    )
```

```python
import functools

import jax
import jax.numpy as jnp
from jax import lax
from jax.experimental import pallas as pl
from jax.experimental.pallas import tpu as pltpu
from jax.sharding import PartitionSpec as P

F32 = jnp.float32
BF16 = jnp.bfloat16


def kernel(
    R, T, H, lr, L, hid, cot, rot, mask, matv, match, out, grad,
    x, w, part, prec, pfull, pfrec, own, gath, matg, upd, updt, gkeep, gsend, yrec, zsend, zrec, fin, frec,
    lsem, psem, rsend, rrecv, msend, mrecv, psend, precv, qsem, asend, arecv, usend, urecv,
    ysend, yrecv, zsem, zrsem, fsem,
):
    q = R // T
    n, F = hid.shape
    C = rot.shape[1]
    S = F // q
    r = lax.axis_index("runs")
    j = lax.axis_index("tp")
    a = r // q
    b = lax.rem(r, q)
    blk = 2 * lr

    def mate(i):
        return i + 1 - 2 * lax.rem(i, 2)

    partner = mate(j)

    def remote(src, dst, ss, rs, dr, dj):
        return pltpu.make_async_remote_copy(
            src_ref=src, dst_ref=dst, send_sem=ss, recv_sem=rs,
            device_id=(dr, dj), device_id_type=pl.DeviceIdType.MESH,
        )

    def other(i, k, size):
        return lax.rem(i + k, size)

    loads = [
        pltpu.make_async_copy(hid, x.at[0], lsem.at[0]),
        pltpu.make_async_copy(cot, x.at[1], lsem.at[1]),
        pltpu.make_async_copy(
            rot.at[pl.ds(pl.multiple_of(j * F, F), F), :],
            w.at[:, pl.ds(pl.multiple_of(j * C, C), C)], lsem.at[2]),
        pltpu.make_async_copy(matv, matg.at[r], lsem.at[3]),
    ]
    for c in loads:
        c.start()

    barrier = pltpu.get_barrier_semaphore()
    for k in range(1, R):
        pl.semaphore_signal(barrier, inc=1, device_id=(other(r, k, R), j),
                            device_id_type=pl.DeviceIdType.MESH)
    for k in range(1, T):
        pl.semaphore_signal(barrier, inc=1, device_id=(r, other(j, k, T)),
                            device_id_type=pl.DeviceIdType.MESH)

    @pl.when(a != j)
    def _():
        pl.semaphore_signal(barrier, inc=1, device_id=(j * q + b, a),
                            device_id_type=pl.DeviceIdType.MESH)
    pl.semaphore_wait(barrier, R - 1 + T - 1 + jnp.where(a != j, 1, 0).astype(jnp.int32))

    def wblock(g, row, size):
        return w.at[pl.ds(pl.multiple_of(row, size), size), pl.ds(pl.multiple_of(g * C, C), C)]

    def rrows(row, size):
        return rot.at[pl.ds(pl.multiple_of(row, size), size), :]

    sub = F // q // 2
    cross = []
    for k in range(1, T // 2):
        same = other(j, 2 * k, T)
        cross.append((same, mate(same)))
    far = [p for pair in cross for p in pair]
    rcopies = []
    for u in range(2):
        for p in far:
            at = b * (2 * sub) + u * sub
            rcopies.append(remote(
                rrows(p * F + at, sub), wblock(j, at, sub),
                rsend.at[p, b, u], rrecv.at[j, b, u], r, p))
    rcopies.append(remote(rrows(partner * F, F), wblock(j, 0, F), psem.at[0], psem.at[1], r, partner))
    for c in rcopies:
        c.start()
    mcopies = []
    for k in range(1, R):
        p = other(r, k, R)
        mcopies.append(remote(matv, matg.at[r], msend.at[p], mrecv.at[r], p, j))
    for c in mcopies:
        c.start()
    for u in range(2):
        for p in far:
            here = wblock(p, b * (2 * sub) + u * sub, sub)
            remote(here, here, rsend.at[p, b, u], rrecv.at[p, b, u], r, p).wait_recv()
            for m in range(1, q):
                e = other(b, m, q)
                c = remote(here, here, rsend.at[p, e, u], rrecv.at[p, b, u], a * q + e, j)
                c.start()
                rcopies.append(c)
    for c in loads:
        c.wait()
    remote(rrows(partner * F, F), wblock(partner, 0, F), psem.at[0], psem.at[1], r, partner).wait_recv()
    for u in range(2):
        for p in far:
            for m in range(1, q):
                e = other(b, m, q)
                here = wblock(p, e * (2 * sub) + u * sub, sub)
                remote(here, here, rsend.at[p, e, u], rrecv.at[p, e, u], a * q + e, j).wait_recv()

    step = L
    pcopies = []
    for s in range(2):
        def body(i, _, s=s):
            rs = pl.ds(pl.multiple_of(i * step, step), step)
            v = jnp.dot(x[s, rs, :], w[...], preferred_element_type=F32)
            ws = pl.ds(pl.multiple_of(s * n + i * step, step), step)
            for p in range(T):
                part[p, ws, :] = v[:, p * C:(p + 1) * C].astype(BF16)
                @pl.when(j == p)
                def _():
                    own[ws, :] = v[:, p * C:(p + 1) * C]
                @pl.when(partner == p)
                def _():
                    pfull[ws, :] = v[:, p * C:(p + 1) * C]
            return 0
        lax.fori_loop(0, n // step, body, 0)
        span = pl.ds(s * n, n)
        for p in far:
            pcopies.append(remote(part.at[p, span], prec.at[j, span], psend.at[p, s], precv.at[j, s], r, p))
            pcopies[-1].start()
        pcopies.append(remote(pfull.at[span], pfrec.at[span], qsem.at[0, s], qsem.at[1, s], r, partner))
        pcopies[-1].start()

    def block(g, s):
        return gath.at[pl.ds(g * blk + s * lr, lr)]

    sends = []
    for s in range(2):
        span = pl.ds(s * n, n)
        for p in far:
            remote(part.at[p, span], prec.at[p, span], psend.at[p, s], precv.at[p, s], r, p).wait_recv()
        remote(pfull.at[span], pfrec.at[span], qsem.at[0, s], qsem.at[1, s], r, partner).wait_recv()
        for i in range(lr):
            rs = pl.ds(s * n + i * L, L)
            v = own[rs, :] + pfrec[rs, :]
            for p in far:
                v = v + prec[p, rs, :].astype(F32)
            if s == 1:
                v = v * mask[pl.ds(i * L, L), :]
            own[rs, :] = v
            gath[r * blk + s * lr + i] = v.astype(BF16)
        for k in range(1, T):
            p = other(a, k, T)
            sends.append(remote(block(r, s), block(r, s), asend.at[p, b, s], arecv.at[r, s], p * q + b, j))
            sends[-1].start()
        for k in range(1, q):
            p = other(b, k, q)
            sends.append(remote(block(r, s), block(r, s), asend.at[a, p, s], arecv.at[r, s], a * q + p, j))
            sends[-1].start()
    for s in range(2):
        for k in range(1, T):
            p = other(a, k, T)
            g = p * q + b
            remote(block(g, s), block(g, s), asend.at[p, b, s], arecv.at[g, s], g, j).wait_recv()
            for m in range(1, q):
                e = other(b, m, q)
                c = remote(block(g, s), block(g, s), asend.at[p, e, s], arecv.at[g, s], a * q + e, j)
                c.start()
                sends.append(c)
    for s in range(2):
        for k in range(T):
            p = other(a, k, T)
            for m in range(1, q):
                g = p * q + other(b, m, q)
                remote(block(g, s), block(g, s), asend.at[p, b, s], arecv.at[g, s], g, j).wait_recv()
    for k in range(1, R):
        p = other(r, k, R)
        remote(matv, matg.at[p], msend.at[p], mrecv.at[p], p, j).wait_recv()

    for i in range(lr):
        rs = pl.ds(i * L, L)
        m = match[i]
        src = gath[m + (m // lr) * lr].astype(F32)
        mine = matg[r, pl.ds(i, 1), :] == (r * lr + i).astype(F32)
        upd[j, rs, :] = jnp.where(mine, 0.0, mask[rs, :] * (src - own[rs, :])).astype(BF16)

        def back(g, acc, i=i):
            for u in range(lr):
                hit = matg[g, pl.ds(u, 1), :] == (r * lr + i).astype(F32)
                acc = acc + jnp.where(hit, gath[g * blk + lr + u].astype(F32), 0.0)
            return acc
        acc = lax.fori_loop(0, R, back, -own[pl.ds((lr + i) * L, L), :])
        for u in range(lr):
            hit = matg[r, pl.ds(u, 1), :] == (r * lr + i).astype(F32)
            full = own[pl.ds((lr + u) * L, L), :]
            acc = acc + jnp.where(hit, full - gath[r * blk + lr + u].astype(F32), 0.0)
        upd[j, pl.ds(n + i * L, L), :] = acc.astype(BF16)

    def pass_on(g, k, way, dj):
        return remote(upd.at[g], upd.at[g], usend.at[way, k], urecv.at[g], r, dj)

    ucopies = [pass_on(j, p, 0, p) for p, _ in cross] + [pass_on(j, partner, 0, partner)]
    for c in ucopies:
        c.start()

    Sh = S // H

    def half(p, e, h):
        fs = pl.ds(pl.multiple_of(e * S + h * Sh, Sh), Sh)
        return (
            jnp.dot(updt[p, :, pl.ds(0, n)], x[1, :, fs], preferred_element_type=F32)
            + jnp.dot(updt[p, :, pl.ds(n, n)], x[0, :, fs], preferred_element_type=F32))

    def ysend_of(p, e, h):
        return remote(gsend.at[p, e, h], yrec.at[b, p, h], ysend.at[p, e, h], yrecv.at[b, p, h], a * q + e, j)

    def grads(p, h):
        for m in range(1, q):
            e = other(b, m, q)
            gsend[p, e, h] = half(p, e, h).astype(BF16)
            ysend_of(p, e, h).start()
        gkeep[p, h] = half(p, b, h)

    def arrive(g):
        pass_on(g, g, 0, j).wait_recv()
        updt[g] = upd[g].T

    updt[j] = upd[j].T
    for h in range(H):
        grads(j, h)
    arrive(partner)
    grads(partner, 0)
    for same, _ in cross:
        pass_on(same, same, 0, j).wait_recv()
        c = pass_on(same, same, 1, partner)
        c.start()
        ucopies.append(c)
        updt[same] = upd[same].T
        grads(same, 0)
    for _, p in cross:
        arrive(p)
        grads(p, 0)
    rest = [partner] + [p for p, _ in cross] + [p for _, p in cross]
    for h in range(1, H):
        for p in rest:
            grads(p, h)

    def inter(i, _):
        rs = pl.ds(pl.multiple_of(i * L, L), L)
        u = jnp.concatenate([upd[p, rs, :] for p in range(T)], axis=1)
        v = lax.dot_general(u, w[...], (((1,), (1,)), ((), ())), preferred_element_type=F32)
        out[rs, :] = (x[0, rs, :].astype(F32) + v).astype(BF16)
        return 0

    def zsend_of(p, h):
        return remote(zsend.at[p, h], zrec.at[a, h], zsem.at[p, h], zrsem.at[a, h], p * q + b, j)

    def ysum(p, h):
        v = gkeep[p, h]
        for m in range(1, q):
            e = other(b, m, q)
            remote(gsend.at[p, e, h], yrec.at[e, p, h], ysend.at[p, e, h], yrecv.at[e, p, h], a * q + e, j).wait_recv()
            v = v + yrec[e, p, h].astype(F32)

        @pl.when(p == a)
        def _():
            fin[h] = v

        @pl.when(p != a)
        def _():
            zsend[p, h] = v.astype(BF16)
            zsend_of(p, h).start()

    def move(h):
        return remote(fin.at[h], frec.at[h], fsem.at[0, h], fsem.at[1, h], j * q + b, a)

    def total(h):
        v = fin[h]
        for k in range(1, T):
            p = other(a, k, T)
            remote(zsend.at[p, h], zrec.at[p, h], zsem.at[p, h], zrsem.at[p, h], p * q + b, j).wait_recv()
            v = v + zrec[p, h].astype(F32)
        fin[h] = v

        @pl.when(a != j)
        def _():
            move(h).start()

    for h in range(H):
        ysum(j, h)
    lax.fori_loop(0, n // L, inter, 0)
    for h in range(H):
        for p in rest:
            ysum(p, h)
        if h:
            total(h - 1)
    total(H - 1)

    for h in range(H):
        @pl.when(a != j)
        def _(h=h):
            move(h).wait()
            grad[pl.ds(h * Sh, Sh), :] = frec[h].T

        @pl.when(a == j)
        def _(h=h):
            grad[pl.ds(h * Sh, Sh), :] = fin[h].T

    for c in rcopies + mcopies + pcopies + sends + ucopies:
        c.wait_send()
    for h in range(H):
        for k in range(T):
            for m in range(1, q):
                ysend_of(other(j, k, T), other(b, m, q), h).wait_send()
        for k in range(1, T):
            zsend_of(other(a, k, T), h).wait_send()


def per_device(R, T, hidden, cotangent, rotation, matching, mask):
    n, F = hidden.shape
    D, C = rotation.shape
    lr, L = mask.shape
    q = R // T
    S = F // q
    H = max(1, min(4, S // 128))
    rows = -(-lr // 8) * 8
    rot = rotation.astype(BF16)
    maskf = jnp.broadcast_to(mask.astype(F32).reshape(n, 1), (n, C))
    matv = jnp.broadcast_to(jnp.pad(matching, (0, rows - lr)).astype(F32)[:, None], (rows, C))
    dma = lambda *s: pltpu.SemaphoreType.DMA(s)
    any_, vm, sm = (pl.BlockSpec(memory_space=m) for m in (pl.ANY, pltpu.VMEM, pltpu.SMEM))
    return pl.pallas_call(
        functools.partial(kernel, R, T, H, lr, L),
        out_shape=(
            jax.ShapeDtypeStruct((n, F), BF16),
            jax.ShapeDtypeStruct((S, C), F32),
        ),
        in_specs=[any_, any_, any_, vm, vm, sm],
        out_specs=(vm, vm),
        scratch_shapes=[
            pltpu.VMEM((2, n, F), BF16),
            pltpu.VMEM((F, T * C), BF16),
            pltpu.VMEM((T, 2 * n, C), BF16),
            pltpu.VMEM((T, 2 * n, C), BF16),
            pltpu.VMEM((2 * n, C), F32),
            pltpu.VMEM((2 * n, C), F32),
            pltpu.VMEM((2 * n, C), F32),
            pltpu.VMEM((R * 2 * lr, L, C), BF16),
            pltpu.VMEM((R, rows, C), F32),
            pltpu.VMEM((T, 2 * n, C), BF16),
            pltpu.VMEM((T, C, 2 * n), BF16),
            pltpu.VMEM((T, H, C, S // H), F32),
            pltpu.VMEM((T, q, H, C, S // H), BF16),
            pltpu.VMEM((q, T, H, C, S // H), BF16),
            pltpu.VMEM((T, H, C, S // H), BF16),
            pltpu.VMEM((T, H, C, S // H), BF16),
            pltpu.VMEM((H, C, S // H), F32),
            pltpu.VMEM((H, C, S // H), F32),
            dma(4), dma(2), dma(T, q, 2), dma(T, q, 2), dma(R), dma(R),
            dma(T, 2), dma(T, 2), dma(2, 2),
            dma(T, q, 2), dma(R, 2), dma(2, T), dma(T),
            dma(T, q, H), dma(q, T, H), dma(T, H), dma(T, H), dma(2, H),
        ],
        compiler_params=pltpu.CompilerParams(
            collective_id=0, has_side_effects=True, vmem_limit_bytes=60 * 1024 * 1024
        ),
    )(hidden, cotangent, rot, maskf, matv, matching)


def solution(mesh):
    in_specs = (P("runs", "tp"), P("runs", "tp"), P(None, "tp"), P("runs"), P("runs", None))
    out_specs = (P("runs", "tp"), P("runs", "tp"))
    return jax.shard_map(
        functools.partial(per_device, mesh.shape["runs"], mesh.shape["tp"]),
        mesh=mesh, in_specs=in_specs, out_specs=out_specs, check_vma=False,
    )
```

```python
import functools

import jax
import jax.numpy as jnp
from jax import lax
from jax.experimental import pallas as pl
from jax.experimental.pallas import tpu as pltpu
from jax.sharding import PartitionSpec as P

F32 = jnp.float32
BF16 = jnp.bfloat16


def kernel(
    R, T, H, lr, L, hid, cot, rot, mask, matv, match, out, grad,
    x, w, part, prec, pfull, pfrec, own, gath, matg, upd, updt, gkeep, gsend, yrec, zsend, zrec, fin, frec,
    lsem, psem, rsend, rrecv, msend, mrecv, psend, precv, qsem, asend, arecv, usend, urecv,
    ysend, yrecv, zsem, zrsem, fsem, hold, hsem, gsem,
):
    q = R // T
    n, F = hid.shape
    C = rot.shape[1]
    S = F // q
    r = lax.axis_index("runs")
    j = lax.axis_index("tp")
    a = r // q
    b = lax.rem(r, q)
    blk = 2 * lr

    def mate(i):
        return i + 1 - 2 * lax.rem(i, 2)

    partner = mate(j)

    def remote(src, dst, ss, rs, dr, dj):
        return pltpu.make_async_remote_copy(
            src_ref=src, dst_ref=dst, send_sem=ss, recv_sem=rs,
            device_id=(dr, dj), device_id_type=pl.DeviceIdType.MESH,
        )

    def other(i, k, size):
        return lax.rem(i + k, size)

    loads = [
        pltpu.make_async_copy(hid, x.at[0], lsem.at[0]),
        pltpu.make_async_copy(cot, x.at[1], lsem.at[1]),
        pltpu.make_async_copy(
            rot.at[pl.ds(pl.multiple_of(j * F, F), F), :],
            w.at[:, pl.ds(pl.multiple_of(j * C, C), C)], lsem.at[2]),
        pltpu.make_async_copy(matv, matg.at[r], lsem.at[3]),
    ]
    for c in loads:
        c.start()

    barrier = pltpu.get_barrier_semaphore()
    for k in range(1, R):
        pl.semaphore_signal(barrier, inc=1, device_id=(other(r, k, R), j),
                            device_id_type=pl.DeviceIdType.MESH)
    for k in range(1, T):
        pl.semaphore_signal(barrier, inc=1, device_id=(r, other(j, k, T)),
                            device_id_type=pl.DeviceIdType.MESH)

    @pl.when(a != j)
    def _():
        pl.semaphore_signal(barrier, inc=1, device_id=(j * q + b, a),
                            device_id_type=pl.DeviceIdType.MESH)
    pl.semaphore_wait(barrier, R - 1 + T - 1 + jnp.where(a != j, 1, 0).astype(jnp.int32))

    def wblock(g, row, size):
        return w.at[pl.ds(pl.multiple_of(row, size), size), pl.ds(pl.multiple_of(g * C, C), C)]

    def rrows(row, size):
        return rot.at[pl.ds(pl.multiple_of(row, size), size), :]

    sub = F // q // 2
    cross = []
    for k in range(1, T // 2):
        same = other(j, 2 * k, T)
        cross.append((same, mate(same)))
    far = [p for pair in cross for p in pair]
    rcopies = []
    for u in range(2):
        for p in far:
            at = b * (2 * sub) + u * sub
            rcopies.append(remote(
                rrows(p * F + at, sub), wblock(j, at, sub),
                rsend.at[p, b, u], rrecv.at[j, b, u], r, p))
    rcopies.append(remote(rrows(partner * F, F), wblock(j, 0, F), psem.at[0], psem.at[1], r, partner))
    for c in rcopies:
        c.start()
    mcopies = []
    for k in range(1, R):
        p = other(r, k, R)
        mcopies.append(remote(matv, matg.at[r], msend.at[p], mrecv.at[r], p, j))
    for c in mcopies:
        c.start()
    for u in range(2):
        for p in far:
            here = wblock(p, b * (2 * sub) + u * sub, sub)
            remote(here, here, rsend.at[p, b, u], rrecv.at[p, b, u], r, p).wait_recv()
            for m in range(1, q):
                e = other(b, m, q)
                c = remote(here, here, rsend.at[p, e, u], rrecv.at[p, b, u], a * q + e, j)
                c.start()
                rcopies.append(c)
    for c in loads:
        c.wait()
    remote(rrows(partner * F, F), wblock(partner, 0, F), psem.at[0], psem.at[1], r, partner).wait_recv()
    for u in range(2):
        for p in far:
            for m in range(1, q):
                e = other(b, m, q)
                here = wblock(p, e * (2 * sub) + u * sub, sub)
                remote(here, here, rsend.at[p, e, u], rrecv.at[p, e, u], a * q + e, j).wait_recv()

    step = L
    pcopies = []
    for s in range(2):
        def body(i, _, s=s):
            rs = pl.ds(pl.multiple_of(i * step, step), step)
            v = jnp.dot(x[s, rs, :], w[...], preferred_element_type=F32)
            ws = pl.ds(pl.multiple_of(s * n + i * step, step), step)
            for p in range(T):
                part[p, ws, :] = v[:, p * C:(p + 1) * C].astype(BF16)
                @pl.when(j == p)
                def _():
                    own[ws, :] = v[:, p * C:(p + 1) * C]
                @pl.when(partner == p)
                def _():
                    pfull[ws, :] = v[:, p * C:(p + 1) * C]
            return 0
        lax.fori_loop(0, n // step, body, 0)
        span = pl.ds(s * n, n)
        for p in far:
            pcopies.append(remote(part.at[p, span], prec.at[j, span], psend.at[p, s], precv.at[j, s], r, p))
            pcopies[-1].start()
        pcopies.append(remote(pfull.at[span], pfrec.at[span], qsem.at[0, s], qsem.at[1, s], r, partner))
        pcopies[-1].start()

    def block(g, s):
        return gath.at[pl.ds(g * blk + s * lr, lr)]

    sends = []
    for s in range(2):
        span = pl.ds(s * n, n)
        for p in far:
            remote(part.at[p, span], prec.at[p, span], psend.at[p, s], precv.at[p, s], r, p).wait_recv()
        remote(pfull.at[span], pfrec.at[span], qsem.at[0, s], qsem.at[1, s], r, partner).wait_recv()
        for i in range(lr):
            rs = pl.ds(s * n + i * L, L)
            v = own[rs, :] + pfrec[rs, :]
            for p in far:
                v = v + prec[p, rs, :].astype(F32)
            if s == 1:
                v = v * mask[pl.ds(i * L, L), :]
            own[rs, :] = v
            gath[r * blk + s * lr + i] = v.astype(BF16)
        for k in range(1, T):
            p = other(a, k, T)
            sends.append(remote(block(r, s), block(r, s), asend.at[p, b, s], arecv.at[r, s], p * q + b, j))
            sends[-1].start()
        for k in range(1, q):
            p = other(b, k, q)
            sends.append(remote(block(r, s), block(r, s), asend.at[a, p, s], arecv.at[r, s], a * q + p, j))
            sends[-1].start()
    for s in range(2):
        for k in range(1, T):
            p = other(a, k, T)
            g = p * q + b
            remote(block(g, s), block(g, s), asend.at[p, b, s], arecv.at[g, s], g, j).wait_recv()
            for m in range(1, q):
                e = other(b, m, q)
                c = remote(block(g, s), block(g, s), asend.at[p, e, s], arecv.at[g, s], a * q + e, j)
                c.start()
                sends.append(c)
    for s in range(2):
        for k in range(T):
            p = other(a, k, T)
            for m in range(1, q):
                g = p * q + other(b, m, q)
                remote(block(g, s), block(g, s), asend.at[p, b, s], arecv.at[g, s], g, j).wait_recv()
    for k in range(1, R):
        p = other(r, k, R)
        remote(matv, matg.at[p], msend.at[p], mrecv.at[p], p, j).wait_recv()

    for i in range(lr):
        rs = pl.ds(i * L, L)
        m = match[i]
        src = gath[m + (m // lr) * lr].astype(F32)
        mine = matg[r, pl.ds(i, 1), :] == (r * lr + i).astype(F32)
        upd[j, rs, :] = jnp.where(mine, 0.0, mask[rs, :] * (src - own[rs, :])).astype(BF16)

        def back(g, acc, i=i):
            for u in range(lr):
                hit = matg[g, pl.ds(u, 1), :] == (r * lr + i).astype(F32)
                acc = acc + jnp.where(hit, gath[g * blk + lr + u].astype(F32), 0.0)
            return acc
        acc = lax.fori_loop(0, R, back, -own[pl.ds((lr + i) * L, L), :])
        for u in range(lr):
            hit = matg[r, pl.ds(u, 1), :] == (r * lr + i).astype(F32)
            full = own[pl.ds((lr + u) * L, L), :]
            acc = acc + jnp.where(hit, full - gath[r * blk + lr + u].astype(F32), 0.0)
        upd[j, pl.ds(n + i * L, L), :] = acc.astype(BF16)

    def pass_on(g, k, way, dj):
        return remote(upd.at[g], upd.at[g], usend.at[way, k], urecv.at[g], r, dj)

    ucopies = [pass_on(j, p, 0, p) for p, _ in cross] + [pass_on(j, partner, 0, partner)]
    for c in ucopies:
        c.start()

    Sh = S // H

    def half(p, e, h):
        fs = pl.ds(pl.multiple_of(e * S + h * Sh, Sh), Sh)
        return (
            jnp.dot(updt[p, :, pl.ds(0, n)], x[1, :, fs], preferred_element_type=F32)
            + jnp.dot(updt[p, :, pl.ds(n, n)], x[0, :, fs], preferred_element_type=F32))

    def ysend_of(p, e, h):
        return remote(gsend.at[p, e, h], yrec.at[b, p, h], ysend.at[p, e, h], yrecv.at[b, p, h], a * q + e, j)

    def grads(p, h):
        for m in range(1, q):
            e = other(b, m, q)
            gsend[p, e, h] = half(p, e, h).astype(BF16)
            ysend_of(p, e, h).start()
        gkeep[p, h] = half(p, b, h)

    def arrive(g):
        pass_on(g, g, 0, j).wait_recv()
        updt[g] = upd[g].T

    updt[j] = upd[j].T
    for h in range(H):
        grads(j, h)
    arrive(partner)
    grads(partner, 0)
    for same, _ in cross:
        pass_on(same, same, 0, j).wait_recv()
        c = pass_on(same, same, 1, partner)
        c.start()
        ucopies.append(c)
        updt[same] = upd[same].T
        grads(same, 0)
    for _, p in cross:
        arrive(p)
        grads(p, 0)
    rest = [partner] + [p for p, _ in cross] + [p for _, p in cross]
    for h in range(1, H):
        for p in rest:
            grads(p, h)

    def inter(i, _):
        rs = pl.ds(pl.multiple_of(i * L, L), L)
        u = jnp.concatenate([upd[p, rs, :] for p in range(T)], axis=1)
        v = lax.dot_general(u, w[...], (((1,), (1,)), ((), ())), preferred_element_type=F32)
        out[rs, :] = (x[0, rs, :].astype(F32) + v).astype(BF16)
        return 0

    def zsend_of(p, h):
        return remote(zsend.at[p, h], zrec.at[a, h], zsem.at[p, h], zrsem.at[a, h], p * q + b, j)

    def ysum(p, h):
        v = gkeep[p, h]
        for m in range(1, q):
            e = other(b, m, q)
            remote(gsend.at[p, e, h], yrec.at[e, p, h], ysend.at[p, e, h], yrecv.at[e, p, h], a * q + e, j).wait_recv()
            v = v + yrec[e, p, h].astype(F32)

        @pl.when(p == a)
        def _():
            fin[h] = v

        @pl.when(p != a)
        def _():
            zsend[p, h] = v.astype(BF16)
            zsend_of(p, h).start()

    def move(h):
        if h % 2 == 0:
            return remote(fin.at[h], hold.at[a, h], fsem.at[0, h], hsem.at[a, h], j * q + b, j)
        return remote(fin.at[h], hold.at[j, h], fsem.at[0, h], hsem.at[j, h], r, a)

    def hand(p, h):
        dr, dj = (r, p) if h % 2 == 0 else (p * q + b, j)
        return remote(hold.at[p, h], frec.at[h], gsem.at[p, h], fsem.at[1, h], dr, dj)

    def relay(h):
        @pl.when(a == j)
        def _():
            for k in range(1, T):
                p = other(a, k, T)
                remote(fin.at[h], hold.at[p, h], fsem.at[0, h], hsem.at[p, h], p * q + b, j).wait_recv()
                hand(p, h).start()

    def total(h):
        v = fin[h]
        for k in range(1, T):
            p = other(a, k, T)
            remote(zsend.at[p, h], zrec.at[p, h], zsem.at[p, h], zrsem.at[p, h], p * q + b, j).wait_recv()
            v = v + zrec[p, h].astype(F32)
        fin[h] = v

        @pl.when(a != j)
        def _():
            move(h).start()

    for h in range(H):
        ysum(j, h)
    lax.fori_loop(0, n // L, inter, 0)
    for h in range(H):
        for p in rest:
            ysum(p, h)
        if h:
            total(h - 1)
        if h > 1:
            relay(h - 2)
    total(H - 1)
    for h in range(max(0, H - 2), H):
        relay(h)

    for h in range(H):
        @pl.when(a != j)
        def _(h=h):
            move(h).wait_send()
            remote(fin.at[h], frec.at[h], fsem.at[0, h], fsem.at[1, h], j * q + b, a).wait_recv()
            grad[pl.ds(h * Sh, Sh), :] = frec[h].T

        @pl.when(a == j)
        def _(h=h):
            grad[pl.ds(h * Sh, Sh), :] = fin[h].T
            for k in range(1, T):
                hand(other(a, k, T), h).wait_send()

    for c in rcopies + mcopies + pcopies + sends + ucopies:
        c.wait_send()
    for h in range(H):
        for k in range(T):
            for m in range(1, q):
                ysend_of(other(j, k, T), other(b, m, q), h).wait_send()
        for k in range(1, T):
            zsend_of(other(a, k, T), h).wait_send()


def per_device(R, T, hidden, cotangent, rotation, matching, mask):
    n, F = hidden.shape
    D, C = rotation.shape
    lr, L = mask.shape
    q = R // T
    S = F // q
    H = max(1, min(4, S // 128))
    rows = -(-lr // 8) * 8
    rot = rotation.astype(BF16)
    maskf = jnp.broadcast_to(mask.astype(F32).reshape(n, 1), (n, C))
    matv = jnp.broadcast_to(jnp.pad(matching, (0, rows - lr)).astype(F32)[:, None], (rows, C))
    dma = lambda *s: pltpu.SemaphoreType.DMA(s)
    any_, vm, sm = (pl.BlockSpec(memory_space=m) for m in (pl.ANY, pltpu.VMEM, pltpu.SMEM))
    return pl.pallas_call(
        functools.partial(kernel, R, T, H, lr, L),
        out_shape=(
            jax.ShapeDtypeStruct((n, F), BF16),
            jax.ShapeDtypeStruct((S, C), F32),
        ),
        in_specs=[any_, any_, any_, vm, vm, sm],
        out_specs=(vm, vm),
        scratch_shapes=[
            pltpu.VMEM((2, n, F), BF16),
            pltpu.VMEM((F, T * C), BF16),
            pltpu.VMEM((T, 2 * n, C), BF16),
            pltpu.VMEM((T, 2 * n, C), BF16),
            pltpu.VMEM((2 * n, C), F32),
            pltpu.VMEM((2 * n, C), F32),
            pltpu.VMEM((2 * n, C), F32),
            pltpu.VMEM((R * 2 * lr, L, C), BF16),
            pltpu.VMEM((R, rows, C), F32),
            pltpu.VMEM((T, 2 * n, C), BF16),
            pltpu.VMEM((T, C, 2 * n), BF16),
            pltpu.VMEM((T, H, C, S // H), F32),
            pltpu.VMEM((T, q, H, C, S // H), BF16),
            pltpu.VMEM((q, T, H, C, S // H), BF16),
            pltpu.VMEM((T, H, C, S // H), BF16),
            pltpu.VMEM((T, H, C, S // H), BF16),
            pltpu.VMEM((H, C, S // H), F32),
            pltpu.VMEM((H, C, S // H), F32),
            dma(4), dma(2), dma(T, q, 2), dma(T, q, 2), dma(R), dma(R),
            dma(T, 2), dma(T, 2), dma(2, 2),
            dma(T, q, 2), dma(R, 2), dma(2, T), dma(T),
            dma(T, q, H), dma(q, T, H), dma(T, H), dma(T, H), dma(2, H),
            pltpu.VMEM((T, H, C, S // H), F32), dma(T, H), dma(T, H),
        ],
        compiler_params=pltpu.CompilerParams(
            collective_id=0, has_side_effects=True, vmem_limit_bytes=60 * 1024 * 1024
        ),
    )(hidden, cotangent, rot, maskf, matv, matching)


def solution(mesh):
    in_specs = (P("runs", "tp"), P("runs", "tp"), P(None, "tp"), P("runs"), P("runs", None))
    out_specs = (P("runs", "tp"), P("runs", "tp"))
    return jax.shard_map(
        functools.partial(per_device, mesh.shape["runs"], mesh.shape["tp"]),
        mesh=mesh, in_specs=in_specs, out_specs=out_specs, check_vma=False,
    )
```
